128 devices in a mesh: batch: 8 (over y_lo, x), corpus: 16 (over z, y_hi, core).
Axes of the slice: x: 4, y: 4 (y_hi: 2, y_lo: 2; y = y_hi * 2 + y_lo), z: 4, core: 2. Of those that a mesh axis runs over, the one named last changes fastest.
Arguments:
- states: bfloat16 [8192, 4096], P('batch', 'corpus'), may hold values from -6 to 6
- norm_gain: float32 [4096], replicated, may hold values from 0.25 to 1.75
- gate_weight: bfloat16 [4096, 12288], P('batch', 'corpus'), may hold values from -0.09375 to 0.09375
- up_weight: bfloat16 [4096, 12288], P('batch', 'corpus'), may hold values from -0.09375 to 0.09375
- down_weight: bfloat16 [12288, 4096], P('corpus', 'batch'), may hold values from -0.0546875 to 0.0546875
- final_gain: float32 [4096], replicated, may hold values from 0.25 to 1.75
- hash_weight: bfloat16 [4096, 1024], replicated, may hold values from -0.75 to 0.75
- query_bits: bfloat16 [4096, 1024], replicated, may hold values from -1 to 1
- slot_map: int32 [128], replicated, may hold values from 0 to 127, each once
- query_index: int32 [4096, 100], replicated, may hold values from 0 to 127
Outputs:
- scores: float32 [4096, 100], P(('batch', 'corpus'))
The draws below stay inside these ranges and needn't reach their ends.
Inputs may be any that keep to these rules, and one draw needn't show every extreme that they name: `slot_map`: each corpus entry is named by exactly one document.
All inputs are finite; a program needn't handle non-finite values.
Results may differ from the reference program's by a relative error of at most 0.017.
Values may be sent and summed in bfloat16 or wider, within the bound.
No kernel may reach another device: no remote copies, remote signals or barrier semaphores. Data moves between devices by JAX's collectives and lax.ppermute only.
A program may use at most 192 MiB of HBM per device.

```python
import jax
import jax.numpy as jnp
from jax import lax

D = 4096
FF = 12288
DOC_LEN = 64
CODE = 1024
NQ = 4096
TOPK = 100
NDOC = 128
TOKENS = 8192
N_CORPUS = 16


def draw_query_bits(key, part):
    picks = jax.random.randint(jax.random.fold_in(key, 7), (NQ, CODE), 0, 2)
    return (2.0 * picks.astype(jnp.float32) - 1.0).astype(jnp.bfloat16)


def plant(entries, stream_key, low, high):
    longest = entries.shape.index(max(entries.shape))
    spots = []
    for shift in (0, 1):
        where = [jax.random.randint(jax.random.fold_in(stream_key, axis), (), 0, length) for axis, length in enumerate(entries.shape)]
        where[longest] = (where[longest] + shift) % entries.shape[longest]
        spots.append(tuple(where))
    return entries.at[spots[0]].set(low).at[spots[1]].set(high)


def steps_of(own_key, shape, cuts, low, largest):
    def one(position, shards_of):
        heights = jax.random.uniform(jax.random.fold_in(jax.random.fold_in(own_key, 6), position), (shards_of,), jnp.float32, low / len(cuts), largest / len(cuts))
        return jnp.repeat(jnp.exp(heights), shape[position] // shards_of).reshape((-1,) + (1,) * (len(shape) - position - 1))

    level = one(*cuts[0])
    for cut in cuts[1:]:
        level = level * one(*cut)
    return level


def scatter_about(stream_key, dims, scale, reach, pieces=(), dtype=jnp.bfloat16):
    result = jax.random.normal(stream_key, dims, jnp.float32) * scale
    if len(pieces) > 0:
        result = steps_of(stream_key, dims, pieces, -0.22, 0.18) * result
    return jnp.clip(result, min=-reach, max=reach).astype(dtype)


def setup_inputs(seed: int = 0) -> dict:
    key_list = jax.random.split(jax.random.key(seed), 11)
    return {
        "states": scatter_about(key_list[0], (TOKENS, D), 1.0, 6.0, ((0, 8), (1, 16))),
        "norm_gain": jnp.clip(1.0 + 0.15 * jax.random.normal(key_list[1], (D,), jnp.float32), 0.25, 1.75),
        "gate_weight": scatter_about(key_list[2], (D, FF), D ** -0.5, 0.09375, ((0, 8), (1, 16))),
        "up_weight": scatter_about(key_list[3], (D, FF), D ** -0.5, 0.09375, ((0, 8), (1, 16))),
        "down_weight": scatter_about(key_list[4], (FF, D), FF ** -0.5, 0.0546875, ((0, 16), (1, 8))),
        "final_gain": jnp.clip(1.0 + 0.15 * jax.random.normal(key_list[5], (D,), jnp.float32), 0.25, 1.75),
        "hash_weight": scatter_about(key_list[6], (D, CODE), (D // 64) ** -0.5, 0.75),
        "query_bits": draw_query_bits(jax.random.fold_in(key_list[10], 71), 0),
        "slot_map": jax.random.permutation(key_list[8], NDOC).astype(jnp.int32),
        "query_index": plant(jax.random.randint(key_list[9], (NQ, TOPK), 0, NDOC), jax.random.fold_in(key_list[9], 1), 0, NDOC - 1).astype(jnp.int32),
    }


def rms(values, gain):
    return values * lax.rsqrt(lax.optimization_barrier(jnp.mean(values * values, axis=-1, keepdims=True)) + 1e-06) * gain

def reference(states, norm_gain, gate_weight, up_weight, down_weight, final_gain, hash_weight, query_bits, slot_map, query_index):
    floats = states.astype(jnp.float32)
    normed = rms(floats, norm_gain).astype(jnp.bfloat16)
    gate = jnp.dot(normed, gate_weight, preferred_element_type=jnp.float32)
    up = jnp.dot(normed, up_weight, preferred_element_type=jnp.float32)
    hidden = (jax.nn.silu(gate) * up).astype(jnp.bfloat16)
    width = FF // N_CORPUS
    hidden_groups = hidden.reshape(TOKENS, N_CORPUS, width).transpose(1, 0, 2)
    down_groups = down_weight.reshape(N_CORPUS, width, D)

    def add_group(total, pair):
        part = jnp.dot(pair[0], pair[1], preferred_element_type=jnp.float32).astype(jnp.bfloat16)
        return (total + part.astype(jnp.float32), None)
    ffn, unused = lax.scan(add_group, jnp.zeros((TOKENS, D), jnp.float32), (hidden_groups, down_groups))
    resid = floats + ffn
    finals = rms(resid, final_gain)
    pooled = lax.optimization_barrier(jnp.mean(finals.reshape(NDOC, DOC_LEN, D), axis=1)).astype(jnp.bfloat16)
    codes = jnp.tanh(jnp.dot(pooled, hash_weight, preferred_element_type=jnp.float32)).astype(jnp.bfloat16)
    corpus = jnp.zeros((NDOC, CODE), jnp.bfloat16).at[slot_map].set(codes)
    table = jnp.dot(query_bits, corpus.T, preferred_element_type=jnp.float32) / jnp.sqrt(jnp.float32(CODE))
    return jnp.take_along_axis(table, query_index, axis=1)
```

```python
import jax
import jax.numpy as jnp
from jax import lax
from jax.sharding import PartitionSpec as P

DOC_LEN = 64
CODE = 1024
NQ = 4096


def side_by_side(arrays, axis, dim, along):
    both = jnp.concatenate(arrays, axis=along)
    whole, at, gathered = (lax.all_gather(both, axis, axis=dim, tiled=True), 0, [])
    for a in arrays:
        gathered.append(lax.slice_in_dim(whole, at, at + a.shape[along], axis=along))
        at += a.shape[along]
    return tuple(gathered)


def rms(values, gain):
    return values * lax.rsqrt(jnp.mean(values * values, axis=-1, keepdims=True) + 1e-06) * gain


def add_rows(left, piece):
    return jnp.dot(left, piece, preferred_element_type=jnp.float32)


def local(
    states,
    norm_gain,
    gate_weight,
    up_weight,
    down_weight,
    final_gain,
    hash_weight,
    query_bits,
    slot_map,
    query_index,
):
    corpus_count = lax.axis_size("corpus")
    devices = lax.axis_size("batch") * corpus_count
    flat_index = lax.axis_index("batch") * corpus_count + lax.axis_index("corpus")
    whole = lax.all_gather(states, "corpus", axis=1, tiled=True)
    normed = rms(whole.astype(jnp.float32), norm_gain).astype(jnp.bfloat16)
    pieces = side_by_side((gate_weight, up_weight), "batch", 0, 1)
    gate = add_rows(normed, pieces[0])
    up = add_rows(normed, pieces[1])
    hidden = (jax.nn.silu(gate) * up).astype(jnp.bfloat16)
    terms = jnp.dot(
        hidden,
        lax.all_gather(down_weight, "batch", axis=1, tiled=True),
        preferred_element_type=jnp.float32,
    )
    ffn = lax.psum_scatter(
        terms.astype(jnp.bfloat16), "corpus", scatter_dimension=0, tiled=True
    ).astype(jnp.float32)
    own_rows = ffn.shape[0]
    mine = lax.dynamic_slice_in_dim(whole, lax.axis_index("corpus") * own_rows, own_rows, 0)
    resid = mine.astype(jnp.float32) + ffn
    finals = rms(resid, final_gain)
    owned_docs = own_rows // DOC_LEN
    pooled = jnp.mean(finals.reshape(owned_docs, DOC_LEN, finals.shape[1]), axis=1).astype(
        jnp.bfloat16
    )
    codes = jnp.tanh(jnp.dot(pooled, hash_weight, preferred_element_type=jnp.float32)).astype(
        jnp.bfloat16
    )
    doc_total = owned_docs * devices
    scale = 1.0 / jnp.sqrt(jnp.float32(CODE))
    gathered = lax.all_to_all(
        jnp.broadcast_to(codes[:, None], (owned_docs, devices, CODE)).reshape(doc_total, CODE),
        ("batch", "corpus"),
        0,
        0,
        tiled=True,
    )
    query_rows = NQ // devices
    my_bits = lax.dynamic_slice_in_dim(query_bits, flat_index * query_rows, query_rows, 0)
    my_index = lax.dynamic_slice_in_dim(query_index, flat_index * query_rows, query_rows, 0)
    table = jnp.dot(my_bits, gathered.T, preferred_element_type=jnp.float32) * scale
    chosen = my_index[:, :, None] == slot_map[None, None, :]
    scores = jnp.sum(jnp.where(chosen, table[:, None, :], 0.0), axis=-1)
    return scores


def solution(mesh):
    placed = (
        P("batch", "corpus"),
        P(),
        P("batch", "corpus"),
        P("batch", "corpus"),
        P("corpus", "batch"),
        P(),
        P(),
        P(),
        P(),
        P(),
    )
    return jax.shard_map(
        local, mesh=mesh, in_specs=placed, out_specs=P(("batch", "corpus"), None), check_vma=False
    )
```

```python
import functools

import jax
import jax.numpy as jnp
from jax import lax
from jax.experimental import pallas as pl
from jax.experimental.pallas import tpu as pltpu
from jax.sharding import PartitionSpec as P

DOC_LEN = 64
CODE = 1024
NQ = 4096
D = 4096
BOTH = ("batch", "corpus")
YLO, NX, NZ, YHI, CORE = 2, 4, 4, 2, 2
DEVICES = YLO * NX * NZ * YHI * CORE
HALF = 384
BLOCK = 512
FIRST = 320


def pairs(dx=0, dy=0, dz=0, dc=0, flip=False):
    out = []
    for s in range(DEVICES):
        ylo, x, z, yhi, c = s // 64, s // 16 % 4, s // 4 % 4, s // 2 % 2, s % 2
        y = (yhi * 2 + ylo + dy) % 4
        lo, hi = y % 2, y // 2
        if flip:
            lo = 1 - lo
        out.append((s, lo * 64 + (x + dx) % 4 * 16 + (z + dz) % 4 * 4 + hi * 2 + (c + dc) % 2))
    return out


def send(a, **to):
    return lax.ppermute(a, BOTH, pairs(**to))


def fetch(a, dx=0, dy=0, dz=0):
    return lax.ppermute(a, BOTH, pairs(dx=-dx, dy=-dy, dz=-dz))


def swap_core(a):
    return send(a, dc=1)


def swap_ylo(a):
    return send(a, flip=True)


def gate_up_kernel(n_x, n_w, x_at, w_at, pos, gain_ref, *refs):
    xs, ws = refs[:n_x], refs[n_x : n_x + n_w]
    out_ref, doc_ref, xv, wv, normed, x_sem, w_sem = refs[n_x + n_w :]
    y, z, x, ylo, core = (pos[i] for i in range(5))
    x_copies, w_copies = [], []
    for (dz, dy, row, k), ref in zip(x_at, xs):
        part = 0
        for i in range(k[0]):
            for j in range(k[1]):
                to = xv.at[lax.rem(z + dz + i, 4), lax.rem(y + dy + j, 4), pl.ds(row, k[2])]
                copy = pltpu.make_async_copy(ref.at[part], to, x_sem.at[len(x_copies)])
                x_copies.append(((dy + j) % 2, copy))
                part += 1
    for (other_lo, dx, other_core, row, size), ref in zip(w_at, ws):
        lo = lax.rem(ylo + other_lo, 2)
        at = (lo * 4 + lax.rem(x + dx, 4)) * BLOCK + row
        to = wv.at[lax.rem(core + other_core, 2), pl.ds(pl.multiple_of(at, 256), size)]
        w_copies.append((other_core, pltpu.make_async_copy(ref, to, w_sem.at[len(w_copies)])))
    for odd in range(2):
        for kind, copy in x_copies:
            if kind == odd:
                copy.start()
        for kind, copy in w_copies:
            if kind == odd:
                copy.start()

    def tile(m, carry):
        lo = lax.rem(ylo + m // 2, 2)
        r = lax.rem(m, 2) * 256
        for odd in range(2):

            @pl.when(m == 2 * odd)
            def _():
                for kind, copy in x_copies:
                    if kind == odd:
                        copy.wait()

        def block(f):
            return xv[f // 2, f % 2 * 2 + lo, pl.ds(pl.multiple_of(r, 256), 256), :].astype(jnp.float32)

        squares = jnp.zeros((256, BLOCK), jnp.float32)
        for f in range(8):
            v = block(f)
            squares += v * v
        total = jnp.sum(squares, axis=-1, keepdims=True)
        factor = lax.rsqrt(total * (1.0 / D) + 1e-06)
        for f in range(8):
            g = gain_ref[:, f * BLOCK : (f + 1) * BLOCK]
            normed[:, f * BLOCK : (f + 1) * BLOCK] = (block(f) * factor * g).astype(jnp.bfloat16)
        first = pl.multiple_of(lo * 512 + r, 256)
        for other_core in range(2):

            @pl.when(m == 0)
            def _():
                for kind, copy in w_copies:
                    if kind == other_core:
                        copy.wait()

            h = lax.rem(core + other_core, 2)
            both = jnp.dot(normed[...], wv[h], preferred_element_type=jnp.float32)
            gate, up = both[:, :HALF], both[:, HALF:]
            out_ref[h, pl.ds(first, 256), :] = (jax.nn.silu(gate) * up).astype(jnp.bfloat16)
        return carry

    lax.fori_loop(0, 4, tile, 0)
    yhi = y // 2
    doc = pl.ds(pl.multiple_of((ylo * 4 + z) * 64, 64), 64)
    for f in range(8):
        doc_ref[:, f * BLOCK : (f + 1) * BLOCK] = xv[f // 2, f % 2 * 2 + yhi, doc, :]


def gate_up(pos, gain, x_pieces, w_pieces):
    x_at, xs = [p[:-1] for p in x_pieces], [p[-1] for p in x_pieces]
    w_at, ws = [p[:-1] for p in w_pieces], [p[-1] for p in w_pieces]
    any_space = pl.BlockSpec(memory_space=pl.ANY)
    n_copies = sum(a[3][0] * a[3][1] for a in x_at)
    return pl.pallas_call(
        functools.partial(gate_up_kernel, len(xs), len(ws), x_at, w_at),
        out_shape=(
            jax.ShapeDtypeStruct((2, 1024, HALF), jnp.bfloat16),
            jax.ShapeDtypeStruct((64, D), jnp.bfloat16),
        ),
        in_specs=[pl.BlockSpec(memory_space=pltpu.SMEM), pl.BlockSpec(memory_space=pltpu.VMEM)]
        + [any_space] * (len(xs) + len(ws)),
        out_specs=(pl.BlockSpec(memory_space=pltpu.VMEM),) * 2,
        scratch_shapes=[
            pltpu.VMEM((4, 4, 512, 512), jnp.bfloat16),
            pltpu.VMEM((2, D, 2 * HALF), jnp.bfloat16),
            pltpu.VMEM((256, D), jnp.bfloat16),
            pltpu.SemaphoreType.DMA((n_copies,)),
            pltpu.SemaphoreType.DMA((len(ws),)),
        ],
        compiler_params=pltpu.CompilerParams(vmem_limit_bytes=40 << 20),
        cost_estimate=pl.CostEstimate(flops=2 * 1024 * D * 4 * HALF, bytes_accessed=24 << 20, transcendentals=1 << 20),
        name="gate_up",
    )(pos, gain, *xs, *ws)


def down_kernel(d_at, by_z, pos, h_ref, *refs):
    n = len(d_at)
    ds, outs = refs[:n], refs[n : n + 4]
    dv, sem = refs[n + 4 :]
    y, z, ylo, core = pos[0], pos[1], pos[3], pos[4]
    copies = []
    for (slot, other_core), ref in zip(d_at, ds):
        for i in range(2):
            h = lax.rem(core + other_core, 2)
            copies.append(
                pltpu.make_async_copy(ref.at[i], dv.at[lax.rem(ylo + i, 2) * 2 + slot, h], sem.at[len(copies)])
            )
    for copy in copies:
        copy.start()
    for copy in copies:
        copy.wait()
    for k, out_ref in zip((2, 1, 3, 0), outs):

        def rows(h):
            if by_z:
                at = lax.rem(z + k, 4) * 64
                return jnp.concatenate(
                    [h_ref[h, pl.ds(pl.multiple_of(at + i * 256, 64), 64), :] for i in range(4)], axis=0
                )
            return h_ref[h, pl.ds(pl.multiple_of(lax.rem(y + k, 4) * 256, 256), 256), :]

        left = [rows(0), rows(1)]
        for b in range(4):
            acc = jnp.dot(left[0], dv[b, 0], preferred_element_type=jnp.float32)
            acc += jnp.dot(left[1], dv[b, 1], preferred_element_type=jnp.float32)
            out_ref[:, b * BLOCK : (b + 1) * BLOCK] = acc.astype(jnp.bfloat16)


def down(pos, hidden, d_pieces, by_z):
    d_at, ds = [p[:-1] for p in d_pieces], [p[-1] for p in d_pieces]
    vmem = pl.BlockSpec(memory_space=pltpu.VMEM)
    return pl.pallas_call(
        functools.partial(down_kernel, d_at, by_z),
        out_shape=(jax.ShapeDtypeStruct((256, 2048), jnp.bfloat16),) * 4,
        in_specs=[pl.BlockSpec(memory_space=pltpu.SMEM), vmem] + [pl.BlockSpec(memory_space=pl.ANY)] * len(ds),
        out_specs=(vmem,) * 4,
        scratch_shapes=[
            pltpu.VMEM((4, 2, HALF, BLOCK), jnp.bfloat16),
            pltpu.SemaphoreType.DMA((2 * len(ds),)),
        ],
        compiler_params=pltpu.CompilerParams(vmem_limit_bytes=20 << 20),
        cost_estimate=pl.CostEstimate(flops=2 * 1024 * 768 * 2048, bytes_accessed=10 << 20, transcendentals=0),
        name="down_z" if by_z else "down_y",
    )(pos, hidden, *ds)


def round_x(block):
    half = block.shape[0] // 2
    near, far = fetch(block, dx=1), fetch(block, dx=3)
    two_a = fetch(near[:half], dx=1)
    two_b = fetch(far[half:], dx=3)
    return ((0, 0, block), (1, 0, near), (3, 0, far), (2, 0, two_a), (2, half, two_b))


def local(states, norm_gain, gate_weight, up_weight, down_weight, final_gain, hash_weight, query_bits, slot_map, query_index):
    batch, corpus = lax.axis_index("batch"), lax.axis_index("corpus")
    ylo, x = batch // 4, batch % 4
    z, yhi, core = corpus // 4, corpus // 2 % 2, corpus % 2
    y = yhi * 2 + ylo
    flat_index = batch * 16 + corpus
    bf16, f32 = jnp.bfloat16, jnp.float32

    own = lax.dynamic_slice(states, (core * 512, 0), (512, 256))
    other = swap_core(lax.dynamic_slice(states, ((1 - core) * 512, 0), (512, 256)))
    tile = jnp.where(core == 0, jnp.concatenate([own, other], 1), jnp.concatenate([other, own], 1))

    def columns(w, half):
        return lax.dynamic_slice(w, (0, half * HALF), (512, HALF))

    w_own = jnp.concatenate([columns(gate_weight, ylo), columns(up_weight, ylo)], 1)
    w_out = jnp.concatenate([columns(gate_weight, 1 - ylo), columns(up_weight, 1 - ylo)], 1)
    d_own = lax.dynamic_slice(down_weight, (ylo * HALF, 0), (HALF, 512))
    d_out = lax.dynamic_slice(down_weight, ((1 - ylo) * HALF, 0), (HALF, 512))

    part_a, part_b = tile[:FIRST], tile[FIRST:]
    line_a = jnp.stack([part_a] + [fetch(part_a, dy=k) for k in (1, 2, 3)])
    line_b = jnp.stack([part_b] + [fetch(part_b, dz=k) for k in (1, 2, 3)])
    w_out, d_out, line_a = lax.optimization_barrier((w_out, d_out, line_a))
    w_other = swap_ylo(w_out)
    rows_b = 512 - FIRST
    near, far = fetch(line_a, dz=1), fetch(line_a, dz=3)
    x_pieces = [
        (0, 0, 0, (1, 4, FIRST), line_a),
        (1, 0, 0, (1, 4, FIRST), near),
        (3, 0, 0, (1, 4, FIRST), far),
        (2, 0, 0, (1, 2, FIRST), fetch(near[:2], dz=1)),
        (2, 2, 0, (1, 2, FIRST), fetch(far[2:], dz=3)),
        (0, 0, FIRST, (4, 1, rows_b), line_b),
    ] + [(0, k, FIRST, (4, 1, rows_b), fetch(line_b, dy=k)) for k in (1, 3, 2)]

    w_pieces = []
    for other_lo, block in enumerate((w_own, w_other)):
        for k, row, piece in round_x(block):
            w_pieces.append((other_lo, k, 0, row, piece.shape[0], piece))
            w_pieces.append((other_lo, k, 1, row, piece.shape[0], swap_core(piece)))

    d_pair = jnp.stack([d_own, swap_ylo(d_out)])
    d_pair, last = lax.optimization_barrier((d_pair, w_pieces[12][-1]))
    w_pieces[12] = w_pieces[12][:-1] + (last,)
    d_all = {k: fetch(d_pair, dx=k) if k else d_pair for k in (0, 1, 3, 2)}
    d_swap = {k: swap_core(d_all[k]) for k in (0, 1, 3, 2)}

    pos = jnp.stack([y, z, x, ylo, core]).astype(jnp.int32)
    hidden, mine = gate_up(pos, norm_gain[None], x_pieces, w_pieces)

    sides = []
    for by_z, ks in ((False, (0, 1)), (True, (2, 3))):
        pieces = [(i, c, side[k]) for i, k in enumerate(ks) for c, side in enumerate((d_all, d_swap))]
        outs = dict(zip((2, 1, 3, 0), down(pos, hidden, pieces, by_z)))
        for k in (2, 1, 3):
            outs[k] = send(outs[k], dz=k) if by_z else send(outs[k], dy=k)
        sides.append(outs)
    terms_a, terms_b = sides

    def chunk(terms, at):
        return sum(lax.dynamic_slice(terms[k], (at * 64, 0), (64, 2048)).astype(f32) for k in range(4))

    ffn_a, ffn_b = chunk(terms_a, z), chunk(terms_b, y)
    got_a, got_b = [], []
    for k in (2, 1, 3):
        got_a.append(send(chunk(terms_a, (z + k) % 4).astype(bf16), dz=k))
        got_b.append(send(chunk(terms_b, (y + k) % 4).astype(bf16), dy=k))
    ffn_a = ffn_a + sum(g.astype(f32) for g in got_a)
    ffn_b = ffn_b + sum(g.astype(f32) for g in got_b)
    ffn = jnp.concatenate([ffn_a.reshape(64, 2, 2, BLOCK), ffn_b.reshape(64, 2, 2, BLOCK)], 2)
    ffn = jnp.roll(ffn, x, axis=2).reshape(64, D)

    resid = mine.astype(f32) + ffn
    finals = resid * lax.rsqrt(jnp.mean(resid * resid, axis=-1, keepdims=True) + 1e-06) * final_gain
    pooled = jnp.mean(finals, axis=0, keepdims=True).astype(bf16)
    codes = jnp.tanh(jnp.dot(pooled, hash_weight, preferred_element_type=f32)).astype(bf16)

    everyone = lax.all_to_all(jnp.broadcast_to(codes, (DEVICES, CODE)), BOTH, 0, 0, tiled=True)
    slots = slot_map.reshape(YHI, NX, CORE, YLO, NZ).transpose(3, 1, 4, 0, 2).reshape(DEVICES)
    rows = NQ // DEVICES
    my_bits = lax.dynamic_slice_in_dim(query_bits, flat_index * rows, rows, 0)
    my_index = lax.dynamic_slice_in_dim(query_index, flat_index * rows, rows, 0)
    scale = 1.0 / jnp.sqrt(f32(CODE))
    table = jnp.dot(my_bits, everyone.T, preferred_element_type=f32) * scale
    chosen = my_index[:, :, None] == slots[None, None, :]
    return jnp.sum(jnp.where(chosen, table[:, None, :], 0.0), axis=-1)


def solution(mesh):
    placed = (
        P("batch", "corpus"),
        P(),
        P("batch", "corpus"),
        P("batch", "corpus"),
        P("corpus", "batch"),
        P(),
        P(),
        P(),
        P(),
        P(),
    )
    return jax.shard_map(
        local, mesh=mesh, in_specs=placed, out_specs=P(BOTH, None), check_vma=False
    )
```
